32 devices in a mesh: groups: 2 (over y), hid: 8 (over z, x), row: 2 (over core).
Axes of the slice: x: 2, y: 2, z: 4, core: 2. Of those that a mesh axis runs over, the one named last changes fastest.
Arguments:
- gate_proj: bfloat16 [32, 32768], P(('groups', 'row'), 'hid'), parts along dimension 0, may hold values from -6 to 6
- up_proj: bfloat16 [32, 32768], P(('groups', 'row'), 'hid'), parts along dimension 0, may hold values from -6 to 6
- hadamard_signs: int32 [32768], P('hid'), may hold values from 0 to 1
- down_codes: bfloat16 [32768, 8192], P('hid', 'row'), may hold values from -127 to 127, as said below
- down_scales: int32 [8192], P('row'), may hold values from 128 to 1279
- residual: bfloat16 [32, 8192], P(('groups', 'hid'), 'row'), parts along dimension 0, may hold values from -16 to 16
- norm_gain: bfloat16 [8192], P('row'), may hold values from 0.099609375 to 1.8984375
- qkv_codes: bfloat16 [8192, 18432], P('row', 'hid'), may hold values from -127 to 127, as said below
- qkv_scales: int32 [18432], P('hid'), may hold values from 128 to 1279
Outputs:
- new_stream: bfloat16 [32, 8192], P(('groups', 'hid'), 'row'), parts along dimension 0
- joined_qkv: bfloat16 [32, 18432], P(('groups', 'row'), 'hid'), parts along dimension 0
The draws below stay inside these ranges and needn't reach their ends.
There are 2 independent parts, one for each index of `groups`. The reference program is written for one: setup_inputs(seed, part) draws one part's arguments, and reference() takes and returns one part's arrays. A program takes and returns all parts, laid end to end along the dimension named above; an argument that names none is the same for every part. Nothing has to cross between parts.
Inputs may be any that keep to these rules, and one draw needn't show every extreme that they name: `down_codes`: every entry is a whole number. `qkv_codes`: every entry is a whole number.
All inputs are finite; a program needn't handle non-finite values.
Results may differ from the reference program's by a relative error of at most 0.0062.
Values may be sent and summed in bfloat16 or wider, within the bound.
A program may use at most 128 MiB of HBM per device.

```python
import math
import jax
import jax.numpy as jnp
from jax import lax

D = 8192
FF = 32768
QKV = 18432
ROWS = 16


def draw_down_codes(key, part):
    return jax.random.randint(jax.random.fold_in(key, 11), (FF, D), -127, 128).astype(jnp.float32).astype(jnp.bfloat16)


def draw_qkv_codes(key, part):
    return jax.random.randint(jax.random.fold_in(key, 23), (D, QKV), -127, 128).astype(jnp.float32).astype(jnp.bfloat16)


def draw_residual(key, part):
    base_key = jax.random.fold_in(key, 37)
    key_noise, key_column = jax.random.split(base_key, 2)
    column_rise = 0.3 * 3.0 ** (jnp.arange(D, dtype=jnp.float32) / D)
    column_spread = jnp.exp(jax.random.uniform(key_column, (D,), jnp.float32, 0.0, math.log(3.3)))
    noise_part = jax.random.truncated_normal(key_noise, -4.0, 4.0, (ROWS, D), jnp.float32)
    values = noise_part * (column_rise * column_spread)[None, :]
    return jnp.clip(values, -16.0, 16.0).astype(jnp.bfloat16)


def place_ends(array, key, smallest, largest):
    place = [jax.random.randint(jax.random.fold_in(key, axis), (), 0, length) for axis, length in enumerate(array.shape)]
    main_axis = array.shape.index(max(array.shape))
    neighbour = place[:main_axis] + [(place[main_axis] + 1) % array.shape[main_axis]] + place[main_axis + 1:]
    return array.at[tuple(place)].set(smallest).at[tuple(neighbour)].set(largest)


def steps_of(own_key, dims, cuts, low, top_value):
    gain = 1.0
    for axis_at, shards_of in cuts:
        steps = jax.random.uniform(jax.random.fold_in(jax.random.fold_in(own_key, 6), axis_at), (shards_of,), jnp.float32, low / len(cuts), top_value / len(cuts))
        gain = gain * jnp.repeat(jnp.exp(steps), dims[axis_at] // shards_of).reshape((-1,) + (1,) * (len(dims) - 1 - axis_at))
    return gain


def normal_values(stream_key, shape, spread, limit, shards=(), held_as=jnp.bfloat16):
    values = jax.random.normal(stream_key, shape, jnp.float32) * spread
    if len(shards) > 0:
        values = steps_of(stream_key, shape, shards, -0.22, 0.18) * values
    return jnp.clip(values, min=-limit, max=limit).astype(held_as)


def setup_inputs(seed: int = 0, part: int = 0) -> dict:
    arg_keys = jax.random.split(jax.random.key(seed), 10)
    part_splits = jax.random.split(jax.random.fold_in(arg_keys[9], part), 10)
    gate_proj = normal_values(part_splits[0], (ROWS, FF), 1.0, 6.0, ((0, 2), (1, 8)))
    up_proj = normal_values(part_splits[1], (ROWS, FF), 1.0, 6.0, ((0, 2), (1, 8)))
    hadamard_signs = place_ends(jax.random.randint(arg_keys[2], (FF,), 0, 2), jax.random.fold_in(arg_keys[2], 1), 0, 1).astype(jnp.int32)
    down_codes = draw_down_codes(jax.random.fold_in(arg_keys[9], 71), part)
    down_scales = place_ends(jax.random.randint(arg_keys[4], (D,), 128, 1280), jax.random.fold_in(arg_keys[4], 1), 128, 1279).astype(jnp.int32)
    residual = draw_residual(jax.random.fold_in(jax.random.fold_in(arg_keys[9], part), 71), part)
    norm_gain = jnp.clip(1.0 + 0.18 * jax.random.normal(arg_keys[6], (D,), jnp.float32), 0.099609375, 1.8984375).astype(jnp.bfloat16)
    qkv_codes = draw_qkv_codes(jax.random.fold_in(arg_keys[9], 71), part)
    qkv_scales = place_ends(jax.random.randint(arg_keys[8], (QKV,), 128, 1280), jax.random.fold_in(arg_keys[8], 1), 128, 1279).astype(jnp.int32)
    return {"gate_proj": gate_proj, "up_proj": up_proj, "hadamard_signs": hadamard_signs, "down_codes": down_codes, "down_scales": down_scales, "residual": residual, "norm_gain": norm_gain, "qkv_codes": qkv_codes, "qkv_scales": qkv_scales}


def sylvester(order_size):
    row_index = lax.broadcasted_iota(jnp.int32, (order_size, order_size), 0)
    column_index = lax.broadcasted_iota(jnp.int32, (order_size, order_size), 1)
    result = jnp.ones((order_size, order_size), jnp.float32)
    for bit_number in range(order_size.bit_length() - 1):
        both_set = row_index // 2 ** bit_number % 2 * (column_index // 2 ** bit_number % 2)
        result = result * (1.0 - 2.0 * both_set.astype(jnp.float32))
    return result

def factor_list(length):
    factors = []
    remain = length
    while remain > 1:
        factor = min(remain, 128)
        factors.append(factor)
        remain = remain // factor
    return factors

def transform_axis(values, order_size, axis_place):
    if order_size == 1:
        return values
    product_moved = jnp.tensordot(values, sylvester(order_size), axes=([axis_place], [0]), precision=lax.Precision.HIGHEST)
    return jnp.moveaxis(product_moved, -1, axis_place)

def transform_last(values):
    factors = factor_list(values.shape[-1])
    leading = values.shape[:-1]
    shaped = values.reshape(leading + tuple(factors))
    for offset, order_size in enumerate(factors):
        shaped = transform_axis(shaped, order_size, len(leading) + offset)
    return shaped.reshape(values.shape)

def reference(gate_proj, up_proj, hadamard_signs, down_codes, down_scales, residual, norm_gain, qkv_codes, qkv_scales):
    hidden = (jax.nn.silu(gate_proj.astype(jnp.float32)) * up_proj.astype(jnp.float32)).astype(jnp.bfloat16)
    flips = (1 - 2 * hadamard_signs).astype(jnp.bfloat16)
    signed = hidden * flips[None, :]
    rotated = (transform_last(signed.astype(jnp.float32)) * (1.0 / math.sqrt(FF))).astype(jnp.bfloat16)
    down = jnp.dot(rotated, down_codes, preferred_element_type=jnp.float32)
    down = down * (down_scales.astype(jnp.float32) * 2.0 ** (-23))[None, :]
    new_stream = (residual.astype(jnp.float32) + down).astype(jnp.bfloat16)
    stream_wide = new_stream.astype(jnp.float32)
    squares = lax.optimization_barrier(jnp.sum(stream_wide * stream_wide, axis=1))
    scaled_rows = (stream_wide * norm_gain.astype(jnp.float32)[None, :]).astype(jnp.bfloat16)
    projected = jnp.dot(scaled_rows, qkv_codes, preferred_element_type=jnp.float32)
    inverse = lax.rsqrt(squares / D + 1e-05)
    joined_qkv = (projected * inverse[:, None] * (qkv_scales.astype(jnp.float32) * 2.0 ** (-22))[None, :]).astype(jnp.bfloat16)
    return (new_stream, joined_qkv)
```

```python
import functools
import math

import jax
import jax.numpy as jnp
from jax import lax
from jax.experimental import pallas as pl
from jax.experimental.pallas import tpu as pltpu
from jax.sharding import PartitionSpec as P

epsilon = 1e-05
F32 = jnp.float32
BF16 = jnp.bfloat16
MESH = pl.DeviceIdType.MESH


def each(count, step, start=0):
    if count - start <= 16:
        for index in range(start, count):
            step(index)
    else:

        def looped(index, carry):
            step(index)
            return carry

        lax.fori_loop(start, count, looped, 0)


def loop(count, step):
    def looped(index, carry):
        step(index)
        return carry

    lax.fori_loop(0, count, looped, 0)


def sylvester(order):
    both = lax.broadcasted_iota(jnp.int32, (order, order), 0) & lax.broadcasted_iota(
        jnp.int32, (order, order), 1
    )
    shift = 1
    while shift < order.bit_length():
        shift *= 2
    while shift > 1:
        shift //= 2
        both = both ^ lax.shift_right_logical(both, shift)
    return (1 - 2 * (both & 1)).astype(F32).astype(BF16)


def tile_of(width, largest):
    tile = largest // 128 * 128
    while width % tile:
        tile -= 128
    return tile


def kernel(
    A, B, J, width_total,
    gate_h, up_h, signs_h, wd_h, dscale_h, res_h, gain_h, wq_h, qscale_h,
    ns_o, out_o,
    gate, up, signs, dscale, res, gain, qscale, wd, wq,
    send1, recv1, xf, send2, recv2, lhsf, lhs, send3, recv3, send4, recv4, rowsf, lhs2, sq, proj,
    send5, recv5,
    in_sem, wd_sem, wq_sem, s1, r1, s2, r2, s3, r3, s4, r4, s5, r5,
):
    h = lax.axis_index("hid")
    r = lax.axis_index("row")
    N = A * B
    me = h * B + r
    Rl, FFl = gate.shape
    q = Rl // A
    R = Rl * B
    S = R // A
    C = wd.shape[2]
    Q = wq.shape[2]

    small = [
        pltpu.make_async_copy(src, dst, in_sem.at[k])
        for k, (src, dst) in enumerate(
            [(gate_h, gate), (up_h, up), (signs_h, signs), (dscale_h, dscale), (res_h, res),
             (gain_h, gain), (qscale_h, qscale)]
        )
    ]
    for copy in small:
        copy.start()

    def wd_copy(j):
        return pltpu.make_async_copy(
            wd_h.at[:, pl.ds(pl.multiple_of(j * C, C), C)], wd.at[j], wd_sem.at[j]
        )

    def wq_copy(j):
        return pltpu.make_async_copy(
            wq_h.at[pl.ds(pl.multiple_of(j * C, C), C), :], wq.at[j], wq_sem.at[j]
        )

    for j in range(J):
        wd_copy(j).start()
    for j in range(J):
        wq_copy(j).start()

    barrier = pltpu.get_barrier_semaphore()

    def greet(t):
        peer = lax.rem(me + t, N)
        pl.semaphore_signal(
            barrier, inc=1, device_id={"hid": lax.div(peer, B), "row": lax.rem(peer, B)},
            device_id_type=MESH,
        )

    each(N, greet, 1)

    for copy in small[:3]:
        copy.wait()
    v = gate[...].astype(F32)
    hidden = (v / (1.0 + jnp.exp(-v)) * up[...].astype(F32)).astype(BF16).astype(F32)
    signed = hidden * (1 - 2 * signs[...]).astype(F32)
    for a in range(A):
        send1[a] = signed[a * q:(a + 1) * q, :].astype(BF16)
    recv1[h] = send1[h]
    pl.semaphore_wait(barrier, N - 1)

    def copy1(t):
        d = lax.rem(h + t, A)
        return pltpu.make_async_remote_copy(
            src_ref=send1.at[d], dst_ref=recv1.at[h], send_sem=s1.at[t - 1], recv_sem=r1.at[t - 1],
            device_id={"hid": d}, device_id_type=MESH,
        )

    each(A, lambda t: copy1(t).start(), 1)
    W = 256
    pieces = FFl // W
    order_right = sylvester(W)
    order_left = sylvester(A * pieces)
    for copy in small[3:]:
        copy.wait()
    each(A, lambda t: copy1(t).wait(), 1)

    for k in range(q):
        for a in range(A):
            xf[a:a + 1, :] = recv1[a, k:k + 1, :].astype(F32)
        stacked = jnp.concatenate(
            [xf[:, p * W:(p + 1) * W] for p in range(pieces)], axis=0
        ).astype(BF16)
        right = jnp.dot(stacked, order_right, preferred_element_type=F32)
        top = right.astype(BF16)
        rest = right - top.astype(F32)
        middle = rest.astype(BF16)
        low = (rest - middle.astype(F32)).astype(BF16)
        both = (
            jnp.dot(order_left, low, preferred_element_type=F32)
            + jnp.dot(order_left, middle, preferred_element_type=F32)
        ) + jnp.dot(order_left, top, preferred_element_type=F32)
        both = both * (1.0 / math.sqrt(FFl * A))
        for p in range(pieces):
            xf[:, p * W:(p + 1) * W] = both[p * A:(p + 1) * A, :]
        for a in range(A):
            send2[a, k:k + 1, :] = xf[a:a + 1, :].astype(BF16)
    recv2[me] = send2[h]

    def copy2(t):
        peer = lax.rem(me + t, N)
        d = lax.div(peer, B)
        return pltpu.make_async_remote_copy(
            src_ref=send2.at[d], dst_ref=recv2.at[me], send_sem=s2.at[t - 1],
            recv_sem=r2.at[t - 1], device_id={"hid": d, "row": lax.rem(peer, B)},
            device_id_type=MESH,
        )

    each(N, lambda t: copy2(t).start(), 1)
    each(N, lambda t: copy2(t).wait(), 1)

    for b in range(B):
        for a in range(A):
            row = b * Rl + a * q
            lhsf[row:row + q, :] = recv2[a * B + b].astype(F32)
    lhs[...] = lhsf[...].astype(BF16)

    def copy3(t, j):
        d = lax.rem(h + t, A)
        return pltpu.make_async_remote_copy(
            src_ref=send3.at[j, d], dst_ref=recv3.at[j, h], send_sem=s3.at[t - 1, j],
            recv_sem=r3.at[t - 1, j], device_id={"hid": d}, device_id_type=MESH,
        )

    def copy4(t, j):
        d = lax.rem(h + t, A)
        return pltpu.make_async_remote_copy(
            src_ref=send4.at[j], dst_ref=recv4.at[j, h], send_sem=s4.at[t - 1, j],
            recv_sem=r4.at[t - 1, j], device_id={"hid": d}, device_id_type=MESH,
        )

    tile = tile_of(C, 512)

    def down_step(j):
        wd_copy(j).wait()
        for n in range(0, C, tile):
            part = jnp.dot(lhs[...], wd[j, :, n:n + tile], preferred_element_type=F32)
            for a in range(A):
                send3[j, a, :, n:n + tile] = part[a * S:(a + 1) * S, :].astype(BF16)
        recv3[j, h] = send3[j, h]
        each(A, lambda t: copy3(t, j).start(), 1)

    loop(J, down_step)

    def stream_step(j):
        each(A, lambda t: copy3(t, j).wait(), 1)
        total = recv3[j, 0].astype(F32)
        for a in range(1, A):
            total = total + recv3[j, a].astype(F32)
        columns = pl.ds(pl.multiple_of(j * C, C), C)
        total = total * (dscale[:, columns].astype(F32) * 2.0 ** (-23))
        stream = (res[:, columns].astype(F32) + total).astype(BF16)
        ns_o[:, columns] = stream
        send4[j] = stream
        recv4[j, h] = stream
        each(A, lambda t: copy4(t, j).start(), 1)

    loop(J, stream_step)

    sq[...] = jnp.zeros_like(sq)
    proj[...] = jnp.zeros_like(proj)
    tile_q = tile_of(Q, 768)

    def project_step(j):
        each(A, lambda t: copy4(t, j).wait(), 1)
        wq_copy(j).wait()
        for a in range(A):
            rowsf[a * S:(a + 1) * S, :] = recv4[j, a].astype(F32)
        wide = rowsf[...]
        columns = pl.ds(pl.multiple_of(j * C, C), C)
        lhs2[...] = (wide * gain[:, columns].astype(F32)).astype(BF16)
        sq[...] += jnp.sum(wide * wide, axis=1, keepdims=True)
        for n in range(0, Q, tile_q):
            proj[:, n:n + tile_q] += jnp.dot(
                lhs2[...], wq[j, :, n:n + tile_q], preferred_element_type=F32
            )

    loop(J, project_step)

    def copy5(t):
        d = lax.rem(r + t, B)
        return pltpu.make_async_remote_copy(
            src_ref=send5.at[d], dst_ref=recv5.at[r], send_sem=s5.at[t - 1],
            recv_sem=r5.at[t - 1], device_id={"row": d}, device_id_type=MESH,
        )

    for b in range(B):
        send5[b, :, :Q] = proj[b * Rl:(b + 1) * Rl, :]
        send5[b, :, Q:] = sq[b * Rl:(b + 1) * Rl, :]
    each(B, lambda t: copy5(t).start(), 1)
    recv5[r] = send5[r]
    each(B, lambda t: copy5(t).wait(), 1)
    total = recv5[0]
    for b in range(1, B):
        total = total + recv5[b]
    inverse = lax.rsqrt(total[:, Q:Q + 1] / width_total + epsilon)
    out_o[...] = (
        total[:, :Q] * inverse * (qscale[...].astype(F32) * 2.0 ** (-22))
    ).astype(BF16)


def body(gate, up, signs, wd, dscale, res, gain, wq, qscale):
    A = lax.axis_size("hid")
    B = lax.axis_size("row")
    N = A * B
    Rl, FFl = gate.shape
    Dl = wd.shape[1]
    Q = wq.shape[1]
    R = Rl * B
    S = res.shape[0]
    q = Rl // A
    J = 4
    C = Dl // J
    any_spec = pl.BlockSpec(memory_space=pl.ANY)
    vmem_spec = pl.BlockSpec(memory_space=pltpu.VMEM)
    dma = pltpu.SemaphoreType.DMA
    call = pl.pallas_call(
        functools.partial(kernel, A, B, J, Dl * B),
        out_shape=(
            jax.ShapeDtypeStruct((S, Dl), BF16),
            jax.ShapeDtypeStruct((Rl, Q), BF16),
        ),
        in_specs=[any_spec] * 9,
        out_specs=(vmem_spec, vmem_spec),
        scratch_shapes=[
            pltpu.VMEM((Rl, FFl), BF16),
            pltpu.VMEM((Rl, FFl), BF16),
            pltpu.VMEM((1, FFl), jnp.int32),
            pltpu.VMEM((1, Dl), jnp.int32),
            pltpu.VMEM((S, Dl), BF16),
            pltpu.VMEM((1, Dl), BF16),
            pltpu.VMEM((1, Q), jnp.int32),
            pltpu.VMEM((J, FFl, C), BF16),
            pltpu.VMEM((J, C, Q), BF16),
            pltpu.VMEM((A, q, FFl), BF16),
            pltpu.VMEM((A, q, FFl), BF16),
            pltpu.VMEM((A, FFl), F32),
            pltpu.VMEM((A, q, FFl), BF16),
            pltpu.VMEM((N, q, FFl), BF16),
            pltpu.VMEM((R, FFl), F32),
            pltpu.VMEM((R, FFl), BF16),
            pltpu.VMEM((J, A, S, C), BF16),
            pltpu.VMEM((J, A, S, C), BF16),
            pltpu.VMEM((J, S, C), BF16),
            pltpu.VMEM((J, A, S, C), BF16),
            pltpu.VMEM((R, C), F32),
            pltpu.VMEM((R, C), BF16),
            pltpu.VMEM((R, 128), F32),
            pltpu.VMEM((R, Q), F32),
            pltpu.VMEM((B, Rl, Q + 128), F32),
            pltpu.VMEM((B, Rl, Q + 128), F32),
            dma((7,)),
            dma((J,)),
            dma((J,)),
            dma((A - 1,)),
            dma((A - 1,)),
            dma((N - 1,)),
            dma((N - 1,)),
            dma((A - 1, J)),
            dma((A - 1, J)),
            dma((A - 1, J)),
            dma((A - 1, J)),
            dma((B - 1,)),
            dma((B - 1,)),
        ],
        compiler_params=pltpu.CompilerParams(
            collective_id=0, has_side_effects=True, vmem_limit_bytes=63 * 1024 * 1024
        ),
    )
    return call(
        gate, up, signs.reshape(1, -1), wd, dscale.reshape(1, -1), res, gain.reshape(1, -1), wq,
        qscale.reshape(1, -1),
    )


def solution(mesh):
    return jax.shard_map(
        body,
        mesh=mesh,
        in_specs=(
            P(("groups", "row"), "hid"),
            P(("groups", "row"), "hid"),
            P("hid"),
            P("hid", "row"),
            P("row"),
            P(("groups", "hid"), "row"),
            P("row"),
            P("row", "hid"),
            P("hid"),
        ),
        out_specs=(P(("groups", "hid"), "row"), P(("groups", "row"), "hid")),
        check_vma=False,
    )
```

```python
import functools
import math

import jax
import jax.numpy as jnp
from jax import lax
from jax.experimental import pallas as pl
from jax.experimental.pallas import tpu as pltpu
from jax.sharding import PartitionSpec as P

epsilon = 1e-05
F32 = jnp.float32
BF16 = jnp.bfloat16
MESH = pl.DeviceIdType.MESH


def each(count, step, start=0):
    if count - start <= 16:
        for index in range(start, count):
            step(index)
    else:

        def looped(index, carry):
            step(index)
            return carry

        lax.fori_loop(start, count, looped, 0)


def loop(count, step):
    def looped(index, carry):
        step(index)
        return carry

    lax.fori_loop(0, count, looped, 0)


def sylvester(order):
    both = lax.broadcasted_iota(jnp.int32, (order, order), 0) & lax.broadcasted_iota(
        jnp.int32, (order, order), 1
    )
    shift = 1
    while shift < order.bit_length():
        shift *= 2
    while shift > 1:
        shift //= 2
        both = both ^ lax.shift_right_logical(both, shift)
    return (1 - 2 * (both & 1)).astype(F32).astype(BF16)


def tile_of(width, largest):
    tile = largest // 128 * 128
    while width % tile:
        tile -= 128
    return tile


def kernel(
    A, B, J, width_total,
    gate_h, up_h, signs_h, wd_h, dscale_h, res_h, gain_h, wq_h, qscale_h,
    ns_o, out_o,
    gate, up, signs, dscale, res, gain1, qscale, wd, wq, gain,
    send1, recv1, xf, send2, recv2, lhsf, lhs, send3, recv3, send4, recv4, rowsf, lhs2, sq, proj,
    send5, recv5,
    in_sem, wd_sem, wq_sem, s1, r1, s2, r2, s3, r3, s4, r4, s5, r5,
):
    h = lax.axis_index("hid")
    r = lax.axis_index("row")
    N = A * B
    me = h * B + r
    Rl, FFl = gate.shape
    q = Rl // A
    R = Rl * B
    S = R // A
    C = wd.shape[2]
    Q = wq.shape[2]

    small = [
        pltpu.make_async_copy(src, dst, in_sem.at[k])
        for k, (src, dst) in enumerate(
            [(gate_h, gate), (up_h, up), (signs_h, signs), (dscale_h, dscale), (res_h, res),
             (gain_h, gain1), (qscale_h, qscale)]
        )
    ]
    for copy in small:
        copy.start()

    def wd_copy(j):
        return pltpu.make_async_copy(
            wd_h.at[:, pl.ds(pl.multiple_of(j * C, C), C)], wd.at[j], wd_sem.at[j]
        )

    def wq_copy(j):
        return pltpu.make_async_copy(
            wq_h.at[pl.ds(pl.multiple_of(j * C, C), C), :], wq.at[j], wq_sem.at[j]
        )

    for j in range(J):
        wd_copy(j).start(priority=1)

    barrier = pltpu.get_barrier_semaphore()

    def greet(t):
        peer = lax.rem(me + t, N)
        pl.semaphore_signal(
            barrier, inc=1, device_id={"hid": lax.div(peer, B), "row": lax.rem(peer, B)},
            device_id_type=MESH,
        )

    each(N, greet, 1)

    for copy in small[:3]:
        copy.wait()
    v = gate[...].astype(F32)
    hidden = (v / (1.0 + jnp.exp(-v)) * up[...].astype(F32)).astype(BF16).astype(F32)
    signed = hidden * (1 - 2 * signs[...]).astype(F32)
    for a in range(A):
        send1[a] = signed[a * q:(a + 1) * q, :].astype(BF16)
    recv1[h] = send1[h]
    pl.semaphore_wait(barrier, N - 1)

    def copy1(t):
        d = lax.rem(h + t, A)
        return pltpu.make_async_remote_copy(
            src_ref=send1.at[d], dst_ref=recv1.at[h], send_sem=s1.at[t - 1], recv_sem=r1.at[t - 1],
            device_id={"hid": d}, device_id_type=MESH,
        )

    each(A, lambda t: copy1(t).start(), 1)
    W = 256
    pieces = FFl // W
    order_right = sylvester(W)
    order_left = sylvester(A * pieces)
    for copy in small[3:]:
        copy.wait()
    gain[...] = gain1[...].astype(F32).reshape(1, -1)
    each(A, lambda t: copy1(t).wait(), 1)

    for k in range(q):
        for a in range(A):
            xf[a:a + 1, :] = recv1[a, k:k + 1, :].astype(F32)
        stacked = jnp.concatenate(
            [xf[:, p * W:(p + 1) * W] for p in range(pieces)], axis=0
        ).astype(BF16)
        right = jnp.dot(stacked, order_right, preferred_element_type=F32)
        top = right.astype(BF16)
        rest = right - top.astype(F32)
        middle = rest.astype(BF16)
        low = (rest - middle.astype(F32)).astype(BF16)
        both = (
            jnp.dot(order_left, low, preferred_element_type=F32)
            + jnp.dot(order_left, middle, preferred_element_type=F32)
        ) + jnp.dot(order_left, top, preferred_element_type=F32)
        both = both * (1.0 / math.sqrt(FFl * A))
        for p in range(pieces):
            xf[:, p * W:(p + 1) * W] = both[p * A:(p + 1) * A, :]
        for a in range(A):
            send2[a, k:k + 1, :] = xf[a:a + 1, :].astype(BF16)
    recv2[me] = send2[h]

    def copy2(t):
        peer = lax.rem(me + t, N)
        d = lax.div(peer, B)
        return pltpu.make_async_remote_copy(
            src_ref=send2.at[d], dst_ref=recv2.at[me], send_sem=s2.at[t - 1],
            recv_sem=r2.at[t - 1], device_id={"hid": d, "row": lax.rem(peer, B)},
            device_id_type=MESH,
        )

    each(N, lambda t: copy2(t).start(), 1)
    each(N, lambda t: copy2(t).wait(), 1)

    for j in range(J):
        wq_copy(j).start(priority=1)
    for b in range(B):
        for a in range(A):
            row = b * Rl + a * q
            lhsf[row:row + q, :] = recv2[a * B + b].astype(F32)
    lhs[...] = lhsf[...].astype(BF16)

    def copy3(t, j):
        d = lax.rem(h + t, A)
        return pltpu.make_async_remote_copy(
            src_ref=send3.at[j, d], dst_ref=recv3.at[j, h], send_sem=s3.at[t - 1, j],
            recv_sem=r3.at[t - 1, j], device_id={"hid": d}, device_id_type=MESH,
        )

    def copy4(t, j):
        d = lax.rem(h + t, A)
        return pltpu.make_async_remote_copy(
            src_ref=send4.at[j], dst_ref=recv4.at[j, h], send_sem=s4.at[t - 1, j],
            recv_sem=r4.at[t - 1, j], device_id={"hid": d}, device_id_type=MESH,
        )

    tile = tile_of(C, 512)

    def down_step(j):
        wd_copy(j).wait()
        for n in range(0, C, tile):
            part = jnp.dot(lhs[...], wd[j, :, n:n + tile], preferred_element_type=F32)
            for a in range(A):
                send3[j, a, :, n:n + tile] = part[a * S:(a + 1) * S, :].astype(BF16)
        recv3[j, h] = send3[j, h]
        each(A, lambda t: copy3(t, j).start(), 1)

    loop(J, down_step)

    def stream_step(j):
        each(A, lambda t: copy3(t, j).wait(), 1)
        total = recv3[j, 0].astype(F32)
        for a in range(1, A):
            total = total + recv3[j, a].astype(F32)
        columns = pl.ds(pl.multiple_of(j * C, C), C)
        total = total * (dscale[:, columns].astype(F32) * 2.0 ** (-23))
        stream = (res[:, columns].astype(F32) + total).astype(BF16)
        ns_o[:, columns] = stream
        send4[j] = stream
        recv4[j, h] = stream
        each(A, lambda t: copy4(t, j).start(), 1)

    loop(J, stream_step)

    sq[...] = jnp.zeros_like(sq)
    proj[...] = jnp.zeros_like(proj)
    tile_q = tile_of(Q, 768)

    def project_step(j):
        each(A, lambda t: copy4(t, j).wait(), 1)
        wq_copy(j).wait()
        for a in range(A):
            rowsf[a * S:(a + 1) * S, :] = recv4[j, a].astype(F32)
        wide = rowsf[...]
        columns = pl.ds(pl.multiple_of(j * C, C), C)
        lhs2[...] = (wide * gain[:, columns]).astype(BF16)
        sq[...] += jnp.sum(wide * wide, axis=1, keepdims=True)
        for n in range(0, Q, tile_q):
            proj[:, n:n + tile_q] += jnp.dot(
                lhs2[...], wq[j, :, n:n + tile_q], preferred_element_type=F32
            )

    loop(J, project_step)

    def copy5(t):
        d = lax.rem(r + t, B)
        return pltpu.make_async_remote_copy(
            src_ref=send5.at[d], dst_ref=recv5.at[r], send_sem=s5.at[t - 1],
            recv_sem=r5.at[t - 1], device_id={"row": d}, device_id_type=MESH,
        )

    for b in range(B):
        send5[b, :, :Q] = proj[b * Rl:(b + 1) * Rl, :]
        send5[b, :, Q:] = sq[b * Rl:(b + 1) * Rl, :]
    each(B, lambda t: copy5(t).start(), 1)
    recv5[r] = send5[r]
    each(B, lambda t: copy5(t).wait(), 1)
    total = recv5[0]
    for b in range(1, B):
        total = total + recv5[b]
    inverse = lax.rsqrt(total[:, Q:Q + 1] / width_total + epsilon)
    out_o[...] = (
        total[:, :Q] * inverse * (qscale[...].astype(F32).reshape(1, Q) * 2.0 ** (-22))
    ).astype(BF16)


def hand_over(ns, out, ns_o, out_o, sem):
    first = pltpu.make_async_copy(ns, ns_o, sem.at[0])
    second = pltpu.make_async_copy(out, out_o, sem.at[1])
    first.start()
    second.start()
    first.wait()
    second.wait()


def body(gate, up, signs, wd, dscale, res, gain, wq, qscale):
    A = lax.axis_size("hid")
    B = lax.axis_size("row")
    N = A * B
    Rl, FFl = gate.shape
    Dl = wd.shape[1]
    Q = wq.shape[1]
    R = Rl * B
    S = res.shape[0]
    q = Rl // A
    J = 4
    C = Dl // J
    any_spec = pl.BlockSpec(memory_space=pl.ANY)
    vmem_spec = pl.BlockSpec(memory_space=pltpu.VMEM)
    dma = pltpu.SemaphoreType.DMA
    call = pl.pallas_call(
        functools.partial(kernel, A, B, J, Dl * B),
        out_shape=(
            jax.ShapeDtypeStruct((S, Dl), BF16),
            jax.ShapeDtypeStruct((Rl, Q), BF16),
        ),
        in_specs=[any_spec] * 9,
        out_specs=(vmem_spec, vmem_spec),
        scratch_shapes=[
            pltpu.VMEM((Rl, FFl), BF16),
            pltpu.VMEM((Rl, FFl), BF16),
            pltpu.VMEM((1, FFl), jnp.int32),
            pltpu.VMEM((1, Dl), jnp.int32),
            pltpu.VMEM((S, Dl), BF16),
            pltpu.VMEM((Dl,), BF16),
            pltpu.VMEM((Q,), jnp.int32),
            pltpu.VMEM((J, FFl, C), BF16),
            pltpu.VMEM((J, C, Q), BF16),
            pltpu.VMEM((1, Dl), F32),
            pltpu.VMEM((A, q, FFl), BF16),
            pltpu.VMEM((A, q, FFl), BF16),
            pltpu.VMEM((A, FFl), F32),
            pltpu.VMEM((A, q, FFl), BF16),
            pltpu.VMEM((N, q, FFl), BF16),
            pltpu.VMEM((R, FFl), F32),
            pltpu.VMEM((R, FFl), BF16),
            pltpu.VMEM((J, A, S, C), BF16),
            pltpu.VMEM((J, A, S, C), BF16),
            pltpu.VMEM((J, S, C), BF16),
            pltpu.VMEM((J, A, S, C), BF16),
            pltpu.VMEM((R, C), F32),
            pltpu.VMEM((R, C), BF16),
            pltpu.VMEM((R, 128), F32),
            pltpu.VMEM((R, Q), F32),
            pltpu.VMEM((B, Rl, Q + 128), F32),
            pltpu.VMEM((B, Rl, Q + 128), F32),
            dma((7,)),
            dma((J,)),
            dma((J,)),
            dma((A - 1,)),
            dma((A - 1,)),
            dma((N - 1,)),
            dma((N - 1,)),
            dma((A - 1, J)),
            dma((A - 1, J)),
            dma((A - 1, J)),
            dma((A - 1, J)),
            dma((B - 1,)),
            dma((B - 1,)),
        ],
        compiler_params=pltpu.CompilerParams(
            collective_id=0, has_side_effects=True, vmem_limit_bytes=63 * 1024 * 1024
        ),
    )
    made = call(
        gate, up, signs.reshape(1, -1), wd, dscale.reshape(1, -1), res, gain, wq,
        qscale,
    )
    return pl.pallas_call(
        hand_over,
        out_shape=(jax.ShapeDtypeStruct((S, Dl), BF16), jax.ShapeDtypeStruct((Rl, Q), BF16)),
        in_specs=[vmem_spec, vmem_spec],
        out_specs=(any_spec, any_spec),
        scratch_shapes=[dma((2,))],
    )(*made)


def solution(mesh):
    return jax.shard_map(
        body,
        mesh=mesh,
        in_specs=(
            P(("groups", "row"), "hid"),
            P(("groups", "row"), "hid"),
            P("hid"),
            P("hid", "row"),
            P("row"),
            P(("groups", "hid"), "row"),
            P("row"),
            P("row", "hid"),
            P("hid"),
        ),
        out_specs=(P(("groups", "hid"), "row"), P(("groups", "row"), "hid")),
        check_vma=False,
    )
```
